256 devices in a mesh: row: 16 (over y, z_lo, core), col: 16 (over z_hi, x).
Axes of the slice: x: 4, y: 4, z: 8 (z_hi: 4, z_lo: 2; z = z_hi * 2 + z_lo), core: 2. Of those that a mesh axis runs over, the one named last changes fastest.
Arguments:
- pairs: bfloat16 [2, 256, 20480], P(None, None, ('row', 'col')), may hold values from -12 to 12
- prior: bfloat16 [2, 20480, 20480], P(None, 'row', 'col'), may hold values from -0.025146484 to 0.025146484
- val_band: int32 [256], replicated, may hold values from 0 to 255
- cond_band: int32 [256], replicated, may hold values from 0 to 2047
- val_energy: float32 [256], replicated, may hold values from -3 to -1
- cond_energy: float32 [2048], replicated, may hold values from 0.5 to 2.5
- coul_root: float32 [20480], replicated, may hold values from 0.3 to 1.5
- potential: float32 [2, 128, 20480], P(None, 'col', 'row'), may hold values from -6 to 6
Outputs:
- screened: float32 [2, 128, 20480], P(None, 'col', 'row')
The draws below stay inside these ranges and needn't reach their ends.
All inputs are finite; a program needn't handle non-finite values.
Results may differ from the reference program's by a relative error of at most 0.0007.
Values may be sent and summed in bfloat16 or wider, within the bound.
No kernel may reach another device: no remote copies, remote signals or barrier semaphores. Data moves between devices by JAX's collectives and lax.ppermute only.
A program may use at most 128 MiB of HBM per device.

```python
import math
import jax
import jax.numpy as jnp
from jax import lax

NG = 20480
NCOL = 128
NV = 256
NC = 2048
PAIRS = 256
ITERS = 2


def plant(result, key, least, top_value):
    shape = result.shape
    spot = [jax.random.randint(jax.random.fold_in(key, axis), (), 0, shape[axis]) for axis in range(len(shape))]
    result = result.at[tuple(spot)].set(least)
    longest = shape.index(max(shape))
    spot[longest] = (spot[longest] + 1) % shape[longest]
    return result.at[tuple(spot)].set(top_value)


def level_of(key, shape, cuts, smallest, high):
    gain, own = 1.0, jax.random.fold_in(key, 6)
    for axis_at, shards_of in cuts:
        steps = jnp.exp(jax.random.uniform(jax.random.fold_in(own, axis_at), (shards_of,), jnp.float32, smallest / len(cuts), high / len(cuts)))
        gain = gain * jnp.repeat(steps, shape[axis_at] // shards_of).reshape([-1 if axis == axis_at else 1 for axis in range(len(shape))])
    return gain


def scatter_about(stream_key, extent, deviation, bound, shards=(), kind=jnp.bfloat16):
    values = deviation * jax.random.normal(stream_key, extent, jnp.float32)
    if shards:
        values = values * level_of(stream_key, extent, shards, -0.22, 0.18)
    return jnp.clip(values, -bound, bound).astype(kind)


def setup_inputs(seed: int = 0) -> dict:
    keys = jax.random.split(jax.random.key(seed), 9)
    return {
        "pairs": scatter_about(keys[0], (2, PAIRS, NG), 2.0, 12.0, ((2, 256),)),
        "prior": scatter_about(keys[1], (2, NG, NG), (0.6 / NG ** 0.5), 0.025146484, ((1, 16), (2, 16))),
        "val_band": plant(jax.random.randint(keys[2], (PAIRS,), 0, NV), jax.random.fold_in(keys[2], 1), 0, NV - 1).astype(jnp.int32),
        "cond_band": plant(jax.random.randint(keys[3], (PAIRS,), 0, NC), jax.random.fold_in(keys[3], 1), 0, NC - 1).astype(jnp.int32),
        "val_energy": jnp.clip(jax.random.uniform(keys[4], (NV,), jnp.float32, -3.0, -1.0), -3.0, -1.0),
        "cond_energy": jnp.clip(jax.random.uniform(keys[5], (NC,), jnp.float32, 0.5, 2.5), 0.5, 2.5),
        "coul_root": jnp.clip(jnp.exp(jax.random.uniform(keys[6], (NG,), jnp.float32, math.log(0.3), math.log(1.5))), 0.3, 1.5),
        "potential": scatter_about(keys[7], (2, NCOL, NG), 1.0, 6.0, ((1, 16), (2, 16)), jnp.float32),
    }


def contract_pairs(first, second):
    return lax.dot_general(first, second, (((0,), (0,)), ((), ())), preferred_element_type=jnp.float32)


def through(scaled_part, matrix):
    return lax.dot_general(scaled_part, matrix, (((1,), (1,)), ((), ())), precision=lax.Precision.HIGHEST, preferred_element_type=jnp.float32)


def reference(pairs, prior, val_band, cond_band, val_energy, cond_energy, coul_root, potential):
    weights = 1.0 / (cond_energy[cond_band] - val_energy[val_band])
    weighted = (weights[None, :, None] * pairs.astype(jnp.float32)).astype(jnp.bfloat16)
    response_real = prior[0].astype(jnp.float32) + (contract_pairs(pairs[0], weighted[0]) + contract_pairs(pairs[1], weighted[1])) / NG
    response_imag = prior[1].astype(jnp.float32) + (contract_pairs(pairs[0], weighted[1]) - contract_pairs(pairs[1], weighted[0])) / NG
    iterate = potential
    for _ in range(ITERS):
        scaled = iterate * coul_root[None, None, :]
        real_part = through(scaled[0], response_real) - through(scaled[1], response_imag)
        imag_part = through(scaled[0], response_imag) + through(scaled[1], response_real)
        applied = iterate + coul_root[None, None, :] * jnp.stack([real_part, imag_part])
        iterate = iterate + 0.5 * (potential - applied)
    return iterate
```

```python
import functools

import jax
import jax.numpy as jnp
from jax import lax
from jax.sharding import PartitionSpec as P

NG = 20480
ITERS = 2
AXES = ("row", "col")


def moves(function):
    pairs = []
    for row in range(16):
        for col in range(16):
            to_row, to_col = function(row, col)
            pairs.append((row * 16 + col, to_row * 16 + to_col))
    return pairs


SWAP = moves(lambda r, c: (c, r))
CORE = moves(lambda r, c: (r ^ 1, c))
NEAR_Z = moves(lambda r, c: (r ^ 2, c))
ALONG_Y = [moves(lambda r, c, s=s: ((r + 4 * s) % 16, c)) for s in range(4)]
ALONG_X = [moves(lambda r, c, s=s: (r, (c & ~3) | ((c + s) & 3))) for s in range(4)]
FAR_Z_SWAP = [moves(lambda r, c, s=s: ((c + 4 * s) % 16, r)) for s in range(4)]


def send(value, pairs):
    return lax.ppermute(value, AXES, pairs)


def pick_energy(band, energy):
    levels = jnp.arange(energy.shape[0], dtype=jnp.int32)
    return jnp.sum(jnp.where(band[:, None] == levels[None, :], energy[None, :], 0.0), axis=1)


def encode(value):
    top = jnp.max(jnp.abs(value), axis=-1, keepdims=True)
    power = jnp.clip(jnp.ceil(jnp.log2(jnp.maximum(top, 1e-35))), -115.0, 125.0)
    scaled = (value * jnp.exp2(-power)).astype(jnp.float16)
    powers = jnp.broadcast_to(power.astype(jnp.float16), value.shape[:-1] + (128,))
    return jnp.concatenate([scaled, powers], axis=-1)


def decode(coded):
    power = coded[..., -128:-127].astype(jnp.float32)
    return coded[..., :-128].astype(jnp.float32) * jnp.exp2(power)


def split(value):
    high = lax.reduce_precision(value, 8, 7)
    return high.astype(jnp.bfloat16), (value - high).astype(jnp.bfloat16)


def ordered_rows(near, position):
    return jnp.where(position == 0, near[0], near[1]), jnp.where(position == 0, near[1], near[0])


def gather_rows(block, row_index):
    core, near_z, along_y = row_index & 1, (row_index >> 1) & 1, row_index >> 2
    other = send(block, NEAR_Z)
    pair = jnp.where(near_z == 0, jnp.stack([block, other]), jnp.stack([other, block]))
    parts = [pair] + [send(pair, ALONG_Y[s]) for s in range(1, 4)]
    ring = jnp.stack(parts)
    ring = jnp.stack([lax.dynamic_index_in_dim(ring, (along_y - y) % 4, 0, keepdims=False) for y in range(4)])
    partner = send(ring, CORE)
    both = jnp.where(core == 0, jnp.stack([ring, partner], 2), jnp.stack([partner, ring], 2))
    return both.reshape((16,) + block.shape)


def dot(left, right, contract):
    return lax.dot_general(left, right, ((contract[0], contract[1]), ((), ())), preferred_element_type=jnp.float32)


def respond(high, low, prior, weighted):
    rows = jnp.concatenate([high, low], axis=0).reshape(512, 1280)

    def product(matrix, axis):
        value = dot(rows, matrix, ((1,), (axis,)))
        value = value.reshape(2, 16, 2, 8, value.shape[-1])
        return value[0] + value[1]

    def complex_product(real_matrix, imag_matrix, axis):
        by_real, by_imag = product(real_matrix, axis), product(imag_matrix, axis)
        real = by_real[:, 0] - by_imag[:, 1]
        imag = by_imag[:, 0] + by_real[:, 1]
        return jnp.concatenate([real, imag], axis=1)

    own = complex_product(prior[0], prior[1], 1)
    paired = complex_product(weighted[0], weighted[1], 0) / NG
    return jnp.concatenate([own, paired], axis=2)


def pair_part(summed, elements):
    high, low = split(summed)
    rows = jnp.concatenate([high, low], axis=0)
    by_real = dot(rows, elements[0], ((1,), (1,)))
    by_imag = dot(rows, elements[1], ((1,), (1,)))
    by_real = by_real[:16] + by_real[16:]
    by_imag = by_imag[:16] + by_imag[16:]
    return jnp.concatenate([by_real[:8] + by_imag[8:], by_real[8:] - by_imag[:8]], axis=0)


def reduce_swap(partial, col_index):
    x, z = col_index & 3, col_index >> 2
    partial = partial.reshape(4, 4, 16, 1536)
    def block_of(s):
        return lax.dynamic_index_in_dim(partial, (x + s) % 4, 1, keepdims=False)
    received = [send(encode(block_of(s)), ALONG_X[s]) for s in range(1, 4)]
    total = block_of(0) + functools.reduce(jnp.add, [decode(part) for part in received])
    coded = encode(total)
    parts = [send(lax.dynamic_index_in_dim(coded, (z + s) % 4, 0, keepdims=False), FAR_Z_SWAP[s]) for s in range(4)]
    return functools.reduce(jnp.add, [decode(part) for part in parts])


def local(pairs, prior, val_band, cond_band, val_energy, cond_energy, coul_root, potential):
    row_index = lax.axis_index("row")
    col_index = lax.axis_index("col")
    weights = 1.0 / (pick_energy(cond_band, cond_energy) - pick_energy(val_band, val_energy))
    gain_row = lax.dynamic_slice_in_dim(coul_root, row_index * 1280, 1280, 0)
    gain = lax.dynamic_slice_in_dim(coul_root, col_index * 1280, 1280, 0)
    scaled = (potential * gain_row).reshape(16, 1280)
    high, low = split(scaled)
    both = jnp.concatenate([high, low], axis=0)
    both = jnp.concatenate([both[:, 256 * q : 256 * q + 256] for q in range(5)], axis=0)
    elements = jnp.swapaxes(pairs, 1, 2).reshape(160, 256)
    block = send(jnp.concatenate([elements, both], axis=0), SWAP)
    start = send(scaled, SWAP)
    whole = gather_rows(block, row_index)
    elements = [whole[:, 80 * k : 80 * k + 80].reshape(1280, 256) for k in range(2)]
    weighted = [(weights[None, :] * part.astype(jnp.float32)).astype(jnp.bfloat16) for part in elements]
    split_rows = whole[:, 160:].reshape(16, 5, 2, 16, 256)
    high, low = [
        jnp.concatenate([split_rows[:, q, k] for q in range(5)], axis=2) for k in range(2)
    ]
    scaled = start
    for step in range(ITERS):
        if step:
            high, low = split(decode(gather_rows(encode(scaled), row_index)))
        partial = respond(high, low, prior, weighted)
        summed = reduce_swap(partial, col_index)
        applied = summed[:, :1280] + pair_part(summed[:, 1280:], elements)
        scaled = scaled + 0.5 * (start - scaled - (gain * gain) * applied)
    result = send(scaled, SWAP)
    return (result / gain_row).reshape(2, 8, 1280)


def solution(mesh):
    in_specs = (
        P(None, None, ("row", "col")),
        P(None, "row", "col"),
        P(),
        P(),
        P(),
        P(),
        P(),
        P(None, "col", "row"),
    )
    out_specs = P(None, "col", "row")
    return jax.shard_map(local, mesh=mesh, in_specs=in_specs, out_specs=out_specs, check_vma=False)
```

```python
import functools

import jax
import jax.numpy as jnp
from jax import lax
from jax.experimental import pallas as pl
from jax.experimental.pallas import tpu as pltpu
from jax.sharding import PartitionSpec as P


NG = 20480
ITERS = 2
FULL = 32000.0
BLOCK = 256
AXES = ("row", "col")


def moves(function):
    pairs = []
    for row in range(16):
        for col in range(16):
            to_row, to_col = function(row, col)
            pairs.append((row * 16 + col, to_row * 16 + to_col))
    return pairs


SWAP = moves(lambda r, c: ((c + 8) % 16, r))
CORE = moves(lambda r, c: (r ^ 1, c))
NEAR_Z = moves(lambda r, c: (r ^ 2, c))
ALONG_Y = [moves(lambda r, c, s=s: ((r + 4 * s) % 16, c)) for s in range(4)]
ALONG_X = [moves(lambda r, c, s=s: (r, (c & ~3) | ((c + s) & 3))) for s in range(4)]
FAR_Z = [moves(lambda r, c, s=s: (r, (c + 4 * s) % 16)) for s in range(4)]
STEPS = (1, 3, 2)


def send(value, pairs):
    return lax.ppermute(value, AXES, pairs)


def pick_energy(band, energy):
    levels = jnp.arange(energy.shape[0], dtype=jnp.int32)
    return jnp.sum(jnp.where(band[:, None] == levels[None, :], energy[None, :], 0.0), axis=1)


def encode(value):
    top = jnp.max(jnp.abs(value), axis=-1, keepdims=True)
    power = jnp.clip(jnp.ceil(jnp.log2(jnp.maximum(top, 1e-30))), -100.0, 125.0)
    scaled = jnp.round(value * (jnp.exp2(-power) * FULL)).astype(jnp.int32).astype(jnp.int16)
    powers = jnp.broadcast_to(power.astype(jnp.int32), value.shape[:-1] + (128,)).astype(jnp.int16)
    return jnp.concatenate([scaled, powers], axis=-1)


def decode(coded):
    power = coded[..., -128:-127].astype(jnp.float32)
    return coded[..., :-128].astype(jnp.float32) * (jnp.exp2(power) * (1.0 / FULL))


def split(value):
    high = lax.reduce_precision(value, 8, 7)
    return high.astype(jnp.bfloat16), (value - high).astype(jnp.bfloat16)


def ring_order(own, pairs, position, turn=0):
    parts = {0: own, **{step: send(own, pairs[step]) for step in STEPS}}
    ring = jnp.stack([parts[step] for step in range(4)])
    return jnp.stack(
        [lax.dynamic_index_in_dim(ring, (position - turn - at) % 4, 0, keepdims=False) for at in range(4)]
    )


def gather_rows(block, row_index):
    core, near_z, along_y = row_index & 1, (row_index >> 1) & 1, row_index >> 2
    other = send(block, NEAR_Z)
    pair = jnp.where(near_z == 0, jnp.stack([block, other]), jnp.stack([other, block]))
    ring = ring_order(pair, ALONG_Y, along_y, turn=2)
    partner = send(ring, CORE)
    both = jnp.where(core == 0, jnp.stack([ring, partner], 2), jnp.stack([partner, ring], 2))
    return both.reshape((16,) + block.shape)


def gather_cols(block, col_index):
    x, z = col_index & 3, col_index >> 2
    column = ring_order(block, FAR_Z, z)
    plane = ring_order(column, ALONG_X, x)
    return jnp.swapaxes(plane, 0, 1).reshape((16,) + block.shape)


def sum_rows(value):
    value = value + send(value, CORE)
    value = value + send(value, NEAR_Z)
    return value + functools.reduce(jnp.add, [send(value, ALONG_Y[step]) for step in STEPS])


def dot(left, right, contract):
    return lax.dot_general(left, right, ((contract[0], contract[1]), ((), ())), preferred_element_type=jnp.float32)


def respond_body(x_ref, coded_ref, prior_ref, own_ref, *refs):
    sent, (high_ref, low_ref, sum_ref) = refs[:3], refs[3:]
    at = pl.program_id(0)

    @pl.when(at == 0)
    def _():
        coded = coded_ref[...].reshape(256, 1408)
        power = coded[:, 1280:].astype(jnp.float32)[:, :1]
        value = coded[:, :1280].astype(jnp.float32) * (jnp.exp2(power) * (1.0 / FULL))
        high = value.astype(jnp.bfloat16)
        high_ref[...] = high
        low_ref[...] = (value - high.astype(jnp.float32)).astype(jnp.bfloat16)

    def product(matrix):
        both = ((1,), (1,))
        value = dot(high_ref[...], matrix, both) + dot(low_ref[...], matrix, both)
        return value.reshape(16, 2, 8, BLOCK)

    by_real, by_imag = product(prior_ref[0]), product(prior_ref[1])
    real = by_real[:, 0] - by_imag[:, 1]
    imag = by_imag[:, 0] + by_real[:, 1]
    place = pl.ds(pl.multiple_of(at * BLOCK, BLOCK), BLOCK)
    sum_ref[:, :, 0:8, place] = real.reshape(4, 4, 8, BLOCK)
    sum_ref[:, :, 8:16, place] = imag.reshape(4, 4, 8, BLOCK)

    @pl.when(at == pl.num_programs(0) - 1)
    def _():
        x = x_ref[0]
        for z in range(4):
            own_ref[z] = sum_ref[z, x]
            for step in range(1, 4):
                value = sum_ref[z, (x + step) & 3]
                top = jnp.max(jnp.abs(value), axis=-1, keepdims=True)
                power = jnp.clip(jnp.ceil(jnp.log2(jnp.maximum(top, 1e-30))), -100.0, 125.0)
                scaled = jnp.round(value * (jnp.exp2(-power) * FULL)).astype(jnp.int32)
                sent[step - 1][z, :, :1280] = scaled.astype(jnp.int16)
                powers = jnp.broadcast_to(power.astype(jnp.int32), (16, 128))
                sent[step - 1][z, :, 1280:] = powers.astype(jnp.int16)


def respond(coded, prior, x):
    whole = lambda *shape: pl.BlockSpec(shape, lambda at: (0,) * len(shape))
    return pl.pallas_call(
        respond_body,
        grid=(1280 // BLOCK,),
        in_specs=[
            pl.BlockSpec(memory_space=pltpu.SMEM),
            whole(16, 16, 1408),
            pl.BlockSpec((2, BLOCK, 1280), lambda at: (0, at, 0)),
        ],
        out_specs=[whole(4, 16, 1280)] + [whole(4, 16, 1408)] * 3,
        out_shape=[jax.ShapeDtypeStruct((4, 16, 1280), jnp.float32)]
        + [jax.ShapeDtypeStruct((4, 16, 1408), jnp.int16)] * 3,
        scratch_shapes=[
            pltpu.VMEM((256, 1280), jnp.bfloat16),
            pltpu.VMEM((256, 1280), jnp.bfloat16),
            pltpu.VMEM((4, 4, 16, 1280), jnp.float32),
        ],
        compiler_params=pltpu.CompilerParams(dimension_semantics=("arbitrary",)),
        cost_estimate=pl.CostEstimate(flops=3400000000, transcendentals=0, bytes_accessed=8000000),
        name="respond",
    )(x.reshape(1), coded, prior)


def project(scaled, weighted):
    high, low = split(scaled)
    value = dot(jnp.concatenate([high, low], axis=0), weighted, ((1,), (0,)))
    value = value[:16] + value[16:]
    real, imag = value[:, :256], value[:, 256:]
    return jnp.concatenate([real[:8] - imag[8:], imag[:8] + real[8:]], axis=0)


def pair_part(summed, elements):
    high, low = split(summed)
    rows = jnp.concatenate([high, low], axis=0)
    by_real = dot(rows, elements[:, :256], ((1,), (1,)))
    by_imag = dot(rows, elements[:, 256:], ((1,), (1,)))
    by_real = by_real[:16] + by_real[16:]
    by_imag = by_imag[:16] + by_imag[16:]
    return jnp.concatenate([by_real[:8] + by_imag[8:], by_real[8:] - by_imag[:8]], axis=0)


def reduce_cols(own, sent, z):
    received = [send(sent[step - 1], ALONG_X[step]) for step in STEPS]
    total = own + functools.reduce(jnp.add, [decode(part) for part in received])
    coded = encode(total)
    received = [send(lax.dynamic_index_in_dim(coded, (z + step) % 4, 0, keepdims=False), FAR_Z[step]) for step in STEPS]
    own = lax.dynamic_index_in_dim(total, z, 0, keepdims=False)
    return own + functools.reduce(jnp.add, [decode(part) for part in received])


def local(pairs, prior, val_band, cond_band, val_energy, cond_energy, coul_root, potential):
    row_index = lax.axis_index("row")
    col_index = lax.axis_index("col")
    gain = lax.dynamic_slice_in_dim(coul_root, row_index * 1280, 1280, 0)
    potential = potential.reshape(16, 1280)
    block = jnp.concatenate([pairs[0].T, pairs[1].T], axis=1)
    iterate = potential
    for step in range(ITERS):
        coded = send(encode(iterate * gain), SWAP)
        if step == 0:
            elements = gather_cols(block, col_index).reshape(1280, 512)
            weights = 1.0 / (pick_energy(cond_band, cond_energy) - pick_energy(val_band, val_energy))
            weights = jnp.concatenate([weights, weights])
            weighted = (weights[None, :] * elements.astype(jnp.float32)).astype(jnp.bfloat16)
        own, *sent = respond(gather_rows(coded, row_index), prior, col_index & 3)
        reduced = reduce_cols(own, sent, col_index >> 2)
        projected = project(iterate * gain, weighted)
        projected = sum_rows(projected) / NG
        applied = gain * (reduced + pair_part(projected, elements))
        iterate = iterate + 0.5 * (potential - iterate - applied)
    return iterate.reshape(2, 8, 1280)


def solution(mesh):
    in_specs = (
        P(None, None, ("row", "col")),
        P(None, "row", "col"),
        P(),
        P(),
        P(),
        P(),
        P(),
        P(None, "col", "row"),
    )
    return jax.shard_map(local, mesh=mesh, in_specs=in_specs, out_specs=P(None, "col", "row"), check_vma=False)
```

```python
import functools

import jax
import jax.numpy as jnp
from jax import lax
from jax.experimental import pallas as pl
from jax.experimental.pallas import tpu as pltpu
from jax.sharding import PartitionSpec as P


NG = 20480
ITERS = 2
FULL = 32000.0
BLOCK = 256
AXES = ("row", "col")


def moves(function):
    pairs = []
    for row in range(16):
        for col in range(16):
            to_row, to_col = function(row, col)
            pairs.append((row * 16 + col, to_row * 16 + to_col))
    return pairs


SWAP = moves(lambda r, c: ((c + 8) % 16, r))
CORE = moves(lambda r, c: (r ^ 1, c))
NEAR_Z = moves(lambda r, c: (r ^ 2, c))
ALONG_Y = [moves(lambda r, c, s=s: ((r + 4 * s) % 16, c)) for s in range(4)]
ALONG_X = [moves(lambda r, c, s=s: (r, (c & ~3) | ((c + s) & 3))) for s in range(4)]
FAR_Z = [moves(lambda r, c, s=s: (r, (c + 4 * s) % 16)) for s in range(4)]
STEPS = (1, 3, 2)


def send(value, pairs):
    return lax.ppermute(value, AXES, pairs)


def pick_energy(band, energy):
    levels = jnp.arange(energy.shape[0], dtype=jnp.int32)
    return jnp.sum(jnp.where(band[:, None] == levels[None, :], energy[None, :], 0.0), axis=1)


def encode(value):
    top = jnp.max(jnp.abs(value), axis=-1, keepdims=True)
    power = jnp.clip(jnp.ceil(jnp.log2(jnp.maximum(top, 1e-30))), -100.0, 125.0)
    scaled = jnp.round(value * (jnp.exp2(-power) * FULL)).astype(jnp.int32).astype(jnp.int16)
    powers = jnp.broadcast_to(power.astype(jnp.int32), value.shape[:-1] + (128,)).astype(jnp.int16)
    return jnp.concatenate([scaled, powers], axis=-1)


def decode(coded):
    power = coded[..., -128:-127].astype(jnp.float32)
    return coded[..., :-128].astype(jnp.float32) * (jnp.exp2(power) * (1.0 / FULL))


def split(value):
    high = lax.reduce_precision(value, 8, 7)
    return high.astype(jnp.bfloat16), (value - high).astype(jnp.bfloat16)


def ring_order(own, pairs, position):
    parts = {0: own, **{step: send(own, pairs[step]) for step in STEPS}}
    ring = jnp.stack([parts[step] for step in range(4)])
    return jnp.stack(
        [lax.dynamic_index_in_dim(ring, (position - at) % 4, 0, keepdims=False) for at in range(4)]
    )


def gather_rows(block):
    pair = jnp.stack([block, send(block, NEAR_Z)])
    parts = {0: pair, **{step: send(pair, ALONG_Y[step]) for step in STEPS}}
    ring = jnp.stack([parts[step] for step in range(4)])
    return ring, send(ring, CORE)


def gather_cols(block, col_index):
    x, z = col_index & 3, col_index >> 2
    column = ring_order(block, FAR_Z, z)
    plane = ring_order(column, ALONG_X, x)
    return jnp.swapaxes(plane, 0, 1).reshape((16,) + block.shape)


def sum_rows(value):
    value = value + send(value, CORE)
    value = value + send(value, NEAR_Z)
    return value + functools.reduce(jnp.add, [send(value, ALONG_Y[step]) for step in STEPS])


def dot(left, right, contract):
    return lax.dot_general(left, right, ((contract[0], contract[1]), ((), ())), preferred_element_type=jnp.float32)


def respond_body(place_ref, own_core_ref, other_core_ref, prior_ref, own_ref, *refs):
    sent, (rows_ref, sum_ref, kept_ref, sems) = refs[:3], refs[3:]
    copies = []
    for at in range(1280 // BLOCK):
        rows = pl.ds(at * BLOCK, BLOCK)
        copies.append(pltpu.make_async_copy(prior_ref.at[:, rows], kept_ref.at[:, rows], sems.at[at]))
        copies[-1].start()
    core, near_z, along_y, x = [place_ref[k] for k in range(4)]
    for k, ref in enumerate((own_core_ref, other_core_ref)):
        for s in range(4):
            for d in range(2):
                coded = ref[s, d]
                power = coded[:, 1280:].astype(jnp.float32)[:, :1]
                value = coded[:, :1280].astype(jnp.float32) * (jnp.exp2(power) * (1.0 / FULL))
                high = value.astype(jnp.bfloat16)
                low = (value - high.astype(jnp.float32)).astype(jnp.bfloat16)
                block = ((along_y - s + 2) & 3) * 4 + ((near_z + d) & 1) * 2 + ((core + k) & 1)
                rows_ref[pl.ds(pl.multiple_of(block * 16, 16), 16), :] = high
                rows_ref[pl.ds(pl.multiple_of(block * 16 + 256, 16), 16), :] = low
    for at in range(0, 1280, BLOCK):
        copies[at // BLOCK].wait()

        def product(part):
            value = dot(rows_ref[...], kept_ref[part, at : at + BLOCK], ((1,), (1,)))
            return (value[:256] + value[256:]).reshape(16, 2, 8, BLOCK)

        by_real, by_imag = product(0), product(1)
        real = by_real[:, 0] - by_imag[:, 1]
        imag = by_imag[:, 0] + by_real[:, 1]
        sum_ref[:, :, 0:8, at : at + BLOCK] = real.reshape(4, 4, 8, BLOCK)
        sum_ref[:, :, 8:16, at : at + BLOCK] = imag.reshape(4, 4, 8, BLOCK)
    for z in range(4):
        own_ref[z] = sum_ref[z, x]
        for step in range(1, 4):
            value = sum_ref[z, (x + step) & 3]
            top = jnp.max(jnp.abs(value), axis=-1, keepdims=True)
            power = jnp.clip(jnp.ceil(jnp.log2(jnp.maximum(top, 1e-30))), -100.0, 125.0)
            scaled = jnp.round(value * (jnp.exp2(-power) * FULL)).astype(jnp.int32)
            sent[step - 1][z, :, :1280] = scaled.astype(jnp.int16)
            powers = jnp.broadcast_to(power.astype(jnp.int32), (16, 128))
            sent[step - 1][z, :, 1280:] = powers.astype(jnp.int16)


def respond(own_core, other_core, prior, place):
    smem, vmem = pl.BlockSpec(memory_space=pltpu.SMEM), pl.BlockSpec(memory_space=pltpu.VMEM)
    return pl.pallas_call(
        respond_body,
        in_specs=[smem, vmem, vmem, pl.BlockSpec(memory_space=pltpu.HBM)],
        out_specs=[vmem] * 4,
        out_shape=[jax.ShapeDtypeStruct((4, 16, 1280), jnp.float32)]
        + [jax.ShapeDtypeStruct((4, 16, 1408), jnp.int16)] * 3,
        scratch_shapes=[
            pltpu.VMEM((512, 1280), jnp.bfloat16),
            pltpu.VMEM((4, 4, 16, 1280), jnp.float32),
            pltpu.VMEM((2, 1280, 1280), jnp.bfloat16),
            pltpu.SemaphoreType.DMA((1280 // BLOCK,)),
        ],
        compiler_params=pltpu.CompilerParams(vmem_limit_bytes=48 << 20),
        cost_estimate=pl.CostEstimate(flops=3400000000, transcendentals=0, bytes_accessed=8000000),
        name="respond",
    )(place, own_core, other_core, prior)


def project(scaled, weighted):
    high, low = split(scaled)
    value = dot(jnp.concatenate([high, low], axis=0), weighted, ((1,), (0,)))
    value = value[:16] + value[16:]
    real, imag = value[:, :256], value[:, 256:]
    return jnp.concatenate([real[:8] - imag[8:], imag[:8] + real[8:]], axis=0)


def pair_part(summed, elements):
    high, low = split(summed)
    rows = jnp.concatenate([high, low], axis=0)
    by_real = dot(rows, elements[:, :256], ((1,), (1,)))
    by_imag = dot(rows, elements[:, 256:], ((1,), (1,)))
    by_real = by_real[:16] + by_real[16:]
    by_imag = by_imag[:16] + by_imag[16:]
    return jnp.concatenate([by_real[:8] + by_imag[8:], by_real[8:] - by_imag[:8]], axis=0)


def reduce_cols(own, sent, z):
    received = [send(sent[step - 1], ALONG_X[step]) for step in STEPS]
    total = own + functools.reduce(jnp.add, [decode(part) for part in received])
    coded = encode(total)
    received = [send(lax.dynamic_index_in_dim(coded, (z + step) % 4, 0, keepdims=False), FAR_Z[step]) for step in STEPS]
    own = lax.dynamic_index_in_dim(total, z, 0, keepdims=False)
    return own + functools.reduce(jnp.add, [decode(part) for part in received])


def local(pairs, prior, val_band, cond_band, val_energy, cond_energy, coul_root, potential):
    row_index = lax.axis_index("row")
    col_index = lax.axis_index("col")
    gain = lax.dynamic_slice_in_dim(coul_root, row_index * 1280, 1280, 0)
    potential = potential.reshape(16, 1280)
    place = jnp.stack([row_index & 1, (row_index >> 1) & 1, row_index >> 2, col_index & 3])
    block = jnp.concatenate([pairs[0].T, pairs[1].T], axis=1)
    iterate = potential
    for step in range(ITERS):
        coded = send(encode(iterate * gain), SWAP)
        if step == 0:
            elements = gather_cols(block, col_index).reshape(1280, 512)
            weights = 1.0 / (pick_energy(cond_band, cond_energy) - pick_energy(val_band, val_energy))
            weights = jnp.concatenate([weights, weights])
            weighted = (weights[None, :] * elements.astype(jnp.float32)).astype(jnp.bfloat16)
        own, *sent = respond(*gather_rows(coded), prior, place)
        reduced = reduce_cols(own, sent, col_index >> 2)
        projected = project(iterate * gain, weighted)
        projected = sum_rows(projected) / NG
        applied = gain * (reduced + pair_part(projected, elements))
        iterate = iterate + 0.5 * (potential - iterate - applied)
    return iterate.reshape(2, 8, 1280)


def solution(mesh):
    in_specs = (
        P(None, None, ("row", "col")),
        P(None, "row", "col"),
        P(),
        P(),
        P(),
        P(),
        P(),
        P(None, "col", "row"),
    )
    return jax.shard_map(local, mesh=mesh, in_specs=in_specs, out_specs=P(None, "col", "row"), check_vma=False)
```

```python
import functools

import jax
import jax.numpy as jnp
from jax import lax
from jax.experimental import pallas as pl
from jax.experimental.pallas import tpu as pltpu
from jax.sharding import PartitionSpec as P


NG = 20480
ITERS = 2
FULL = 32000.0
BLOCK = 256
AXES = ("row", "col")


def moves(function):
    pairs = []
    for row in range(16):
        for col in range(16):
            to_row, to_col = function(row, col)
            pairs.append((row * 16 + col, to_row * 16 + to_col))
    return pairs


SWAP = moves(lambda r, c: ((c + 8) % 16, r))
CORE = moves(lambda r, c: (r ^ 1, c))
NEAR_Z = moves(lambda r, c: (r ^ 2, c))
ALONG_Y = [moves(lambda r, c, s=s: ((r + 4 * s) % 16, c)) for s in range(4)]
ALONG_X = [moves(lambda r, c, s=s: (r, (c & ~3) | ((c + s) & 3))) for s in range(4)]
FAR_Z = [moves(lambda r, c, s=s: (r, (c + 4 * s) % 16)) for s in range(4)]
STEPS = (1, 3, 2)


def send(value, pairs):
    return lax.ppermute(value, AXES, pairs)


def pick_energy(band, energy):
    levels = jnp.arange(energy.shape[0], dtype=jnp.int32)
    return jnp.sum(jnp.where(band[:, None] == levels[None, :], energy[None, :], 0.0), axis=1)


def encode(value):
    top = jnp.max(jnp.abs(value), axis=-1, keepdims=True)
    power = jnp.clip(jnp.ceil(jnp.log2(jnp.maximum(top, 1e-30))), -100.0, 125.0)
    scaled = jnp.round(value * (jnp.exp2(-power) * FULL)).astype(jnp.int32).astype(jnp.int16)
    powers = jnp.broadcast_to(power.astype(jnp.int32), value.shape[:-1] + (128,)).astype(jnp.int16)
    return jnp.concatenate([scaled, powers], axis=-1)


def decode(coded):
    power = coded[..., -128:-127].astype(jnp.float32)
    return coded[..., :-128].astype(jnp.float32) * (jnp.exp2(power) * (1.0 / FULL))


def split(value):
    high = lax.reduce_precision(value, 8, 7)
    return high.astype(jnp.bfloat16), (value - high).astype(jnp.bfloat16)


def ring_order(own, pairs, position):
    parts = {0: own, **{step: send(own, pairs[step]) for step in STEPS}}
    ring = jnp.stack([parts[step] for step in range(4)])
    return jnp.stack(
        [lax.dynamic_index_in_dim(ring, (position - at) % 4, 0, keepdims=False) for at in range(4)]
    )


def gather_rows(block):
    pair = jnp.stack([block, send(block, NEAR_Z)])
    parts = {0: pair, **{step: send(pair, ALONG_Y[step]) for step in STEPS}}
    ring = jnp.stack([parts[step] for step in range(4)])
    return ring, send(ring, CORE)


def gather_cols(block, col_index):
    x, z = col_index & 3, col_index >> 2
    column = ring_order(block, FAR_Z, z)
    plane = ring_order(column, ALONG_X, x)
    return jnp.swapaxes(plane, 0, 1).reshape((16,) + block.shape)


def sum_rows(value):
    value = value + send(value, CORE)
    value = value + send(value, NEAR_Z)
    return value + functools.reduce(jnp.add, [send(value, ALONG_Y[step]) for step in STEPS])


def dot(left, right, contract):
    return lax.dot_general(left, right, ((contract[0], contract[1]), ((), ())), preferred_element_type=jnp.float32)


def respond_body(place_ref, own_core_ref, other_core_ref, gain_ref, prior_ref, own_ref, *refs):
    sent, (rows_ref, sum_ref, kept_ref, sems) = refs[:3], refs[3:]
    copies = []
    for at in range(1280 // BLOCK):
        rows = pl.ds(at * BLOCK, BLOCK)
        copies.append(pltpu.make_async_copy(prior_ref.at[:, rows], kept_ref.at[:, rows], sems.at[at]))
        copies[-1].start()
    core, near_z, along_y, x = [place_ref[k] for k in range(4)]
    for k, ref in enumerate((own_core_ref, other_core_ref)):
        for s in range(4):
            for d in range(2):
                coded = ref[s, d]
                power = coded[:, 1280:].astype(jnp.float32)[:, :1]
                value = coded[:, :1280].astype(jnp.float32) * (jnp.exp2(power) * (1.0 / FULL)) * gain_ref[...]
                high = value.astype(jnp.bfloat16)
                low = (value - high.astype(jnp.float32)).astype(jnp.bfloat16)
                block = ((along_y - s + 2) & 3) * 4 + ((near_z + d) & 1) * 2 + ((core + k) & 1)
                rows_ref[pl.ds(pl.multiple_of(block * 16, 16), 16), :] = high
                rows_ref[pl.ds(pl.multiple_of(block * 16 + 256, 16), 16), :] = low
    for at in range(0, 1280, BLOCK):
        copies[at // BLOCK].wait()

        def product(part):
            value = dot(rows_ref[...], kept_ref[part, at : at + BLOCK], ((1,), (1,)))
            return (value[:256] + value[256:]).reshape(16, 2, 8, BLOCK)

        by_real, by_imag = product(0), product(1)
        real = by_real[:, 0] - by_imag[:, 1]
        imag = by_imag[:, 0] + by_real[:, 1]
        sum_ref[:, :, 0:8, at : at + BLOCK] = real.reshape(4, 4, 8, BLOCK)
        sum_ref[:, :, 8:16, at : at + BLOCK] = imag.reshape(4, 4, 8, BLOCK)
    for z in range(4):
        own_ref[z] = sum_ref[z, x]
        for step in range(1, 4):
            value = sum_ref[z, (x + step) & 3]
            top = jnp.max(jnp.abs(value), axis=-1, keepdims=True)
            power = jnp.clip(jnp.ceil(jnp.log2(jnp.maximum(top, 1e-30))), -100.0, 125.0)
            scaled = jnp.round(value * (jnp.exp2(-power) * FULL)).astype(jnp.int32)
            sent[step - 1][z, :, :1280] = scaled.astype(jnp.int16)
            powers = jnp.broadcast_to(power.astype(jnp.int32), (16, 128))
            sent[step - 1][z, :, 1280:] = powers.astype(jnp.int16)


def respond(own_core, other_core, gain, prior, place):
    smem, vmem = pl.BlockSpec(memory_space=pltpu.SMEM), pl.BlockSpec(memory_space=pltpu.VMEM)
    return pl.pallas_call(
        respond_body,
        in_specs=[smem, vmem, vmem, vmem, pl.BlockSpec(memory_space=pltpu.HBM)],
        out_specs=[vmem] * 4,
        out_shape=[jax.ShapeDtypeStruct((4, 16, 1280), jnp.float32)]
        + [jax.ShapeDtypeStruct((4, 16, 1408), jnp.int16)] * 3,
        scratch_shapes=[
            pltpu.VMEM((512, 1280), jnp.bfloat16),
            pltpu.VMEM((4, 4, 16, 1280), jnp.float32),
            pltpu.VMEM((2, 1280, 1280), jnp.bfloat16),
            pltpu.SemaphoreType.DMA((1280 // BLOCK,)),
        ],
        compiler_params=pltpu.CompilerParams(vmem_limit_bytes=48 << 20),
        cost_estimate=pl.CostEstimate(flops=3400000000, transcendentals=0, bytes_accessed=8000000),
        name="respond",
    )(place, own_core, other_core, gain, prior)


def prepare_body(value_ref, coded_ref):
    value = value_ref[...]
    top = jnp.max(jnp.abs(value), axis=-1, keepdims=True)
    power = jnp.clip(jnp.ceil(jnp.log2(jnp.maximum(top, 1e-30))), -100.0, 125.0)
    scaled = jnp.round(value * (jnp.exp2(-power) * FULL)).astype(jnp.int32)
    coded_ref[:, :1280] = scaled.astype(jnp.int16)
    coded_ref[:, 1280:] = jnp.broadcast_to(power.astype(jnp.int32), (16, 128)).astype(jnp.int16)


def prepare(value):
    vmem = pl.BlockSpec(memory_space=pltpu.VMEM)
    return pl.pallas_call(
        prepare_body,
        in_specs=[vmem],
        out_specs=vmem,
        out_shape=jax.ShapeDtypeStruct((16, 1408), jnp.int16),
        compiler_params=pltpu.CompilerParams(vmem_limit_bytes=8 << 20),
        name="prepare",
    )(value)


def project(scaled, weighted):
    high, low = split(scaled)
    value = dot(jnp.concatenate([high, low], axis=0), weighted, ((1,), (0,)))
    value = value[:16] + value[16:]
    real, imag = value[:, :256], value[:, 256:]
    return jnp.concatenate([real[:8] - imag[8:], imag[:8] + real[8:]], axis=0)


def pair_part(summed, elements):
    high, low = split(summed)
    rows = jnp.concatenate([high, low], axis=0)
    by_real = dot(rows, elements[:, :256], ((1,), (1,)))
    by_imag = dot(rows, elements[:, 256:], ((1,), (1,)))
    by_real = by_real[:16] + by_real[16:]
    by_imag = by_imag[:16] + by_imag[16:]
    return jnp.concatenate([by_real[:8] + by_imag[8:], by_real[8:] - by_imag[:8]], axis=0)


def reduce_cols(own, sent, z):
    received = [send(sent[step - 1], ALONG_X[step]) for step in STEPS]
    total = own + functools.reduce(jnp.add, [decode(part) for part in received])
    coded = encode(total)
    received = [send(lax.dynamic_index_in_dim(coded, (z + step) % 4, 0, keepdims=False), FAR_Z[step]) for step in STEPS]
    own = lax.dynamic_index_in_dim(total, z, 0, keepdims=False)
    return own + functools.reduce(jnp.add, [decode(part) for part in received])


def local(pairs, prior, val_band, cond_band, val_energy, cond_energy, coul_root, potential):
    row_index = lax.axis_index("row")
    col_index = lax.axis_index("col")
    gain = lax.dynamic_slice_in_dim(coul_root, row_index * 1280, 1280, 0)
    potential = potential.reshape(16, 1280)
    place = jnp.stack([row_index & 1, (row_index >> 1) & 1, row_index >> 2, col_index & 3])
    block = jnp.concatenate([pairs[0].T, pairs[1].T], axis=1)
    iterate = potential
    for step in range(ITERS):
        coded = send(encode(iterate) if step else prepare(iterate), SWAP)
        if step == 0:
            elements = gather_cols(block, col_index).reshape(1280, 512)
            weights = 1.0 / (pick_energy(cond_band, cond_energy) - pick_energy(val_band, val_energy))
            weights = jnp.concatenate([weights, weights])
            gain_col = lax.dynamic_slice_in_dim(coul_root, col_index * 1280, 1280, 0).reshape(1, 1280)
            weighted = (weights[None, :] * elements.astype(jnp.float32)).astype(jnp.bfloat16)
        own, *sent = respond(*gather_rows(coded), gain_col, prior, place)
        reduced = reduce_cols(own, sent, col_index >> 2)
        projected = project(iterate * gain, weighted)
        projected = sum_rows(projected) / NG
        applied = gain * (reduced + pair_part(projected, elements))
        iterate = iterate + 0.5 * (potential - iterate - applied)
    return iterate.reshape(2, 8, 1280)


def solution(mesh):
    in_specs = (
        P(None, None, ("row", "col")),
        P(None, "row", "col"),
        P(),
        P(),
        P(),
        P(),
        P(),
        P(None, "col", "row"),
    )
    return jax.shard_map(local, mesh=mesh, in_specs=in_specs, out_specs=P(None, "col", "row"), check_vma=False)
```
